32 devices in a mesh: grp: 2 (over x), chol: 16 (over z, y, core).
Axes of the slice: x: 2, y: 2, z: 4, core: 2. Of those that a mesh axis runs over, the one named last changes fastest.
Arguments:
- chol_full: bfloat16 [128, 1024, 1024], P(None, 'chol'), may hold values from -0.015625 to 0.015625
- chol_half: bfloat16 [128, 1024, 256], P(None, 'chol'), may hold values from -0.046875 to 0.046875
- green: bfloat16 [128, 1024, 256], P('grp', 'chol'), parts along dimension 0, may hold values from -6 to 6
- gauss: float32 [128, 128], P('grp'), parts along dimension 0, may hold values from -5 to 5
- orbitals: bfloat16 [128, 1024, 256], P(('grp', 'chol')), parts along dimension 0, may hold values from -6 to 6
Outputs:
- new_orbitals: bfloat16 [128, 1024, 256], P(('grp', 'chol')), parts along dimension 0
- log_factor: float32 [128], P(('grp', 'chol')), parts along dimension 0
The draws below stay inside these ranges and needn't reach their ends.
There are 2 independent parts, one for each index of `grp`. The reference program is written for one: setup_inputs(seed, part) draws one part's arguments, and reference() takes and returns one part's arrays. A program takes and returns all parts, laid end to end along the dimension named above; an argument that names none is the same for every part. Nothing has to cross between parts.
All inputs are finite; a program needn't handle non-finite values.
Results may differ from the reference program's by a relative error of at most 0.0032.
Values may be sent and summed in bfloat16 or wider, within the bound.
A program may use at most 128 MiB of HBM per device.

```python
import jax
import jax.numpy as jnp
from jax import lax

N = 1024
NOCC = 256
NCH = 128
WALKERS = 64


def raised(drawn, own_key, source, target, parts, factor):
    def block_of(dim):
        return (jnp.arange(drawn.shape[dim]) // (drawn.shape[dim] // parts)).reshape((-1,) + (1,) * (drawn.ndim - 1 - dim))

    one_side = jax.random.permutation(own_key, parts)[block_of(target)]
    other_side = (block_of(target) + parts // 2) % parts
    return jnp.where((block_of(source) == one_side) | (block_of(source) == other_side), factor * drawn, drawn)


def block_scale(rng, dims, shards, smallest, high):
    loudness = 1.0
    for position, blocks in shards:
        steps = jax.random.uniform(jax.random.fold_in(jax.random.fold_in(rng, 6), position), (blocks,), jnp.float32, smallest / len(shards), high / len(shards))
        loudness = loudness * jnp.repeat(jnp.exp(steps), dims[position] // blocks).reshape((-1,) + (1,) * (len(dims) - 1 - position))
    return loudness


def bell_draw(own_key, dims, spread, limit, cuts=(), dtype=jnp.bfloat16):
    entries = spread * jax.random.normal(own_key, dims, jnp.float32)
    if cuts:
        entries = entries * block_scale(own_key, dims, cuts, -0.22, 0.18)
    return jnp.clip(entries, -limit, limit).astype(dtype)


def noise_with(key, dims, deviation, most, shards, heavy, kind=jnp.bfloat16):
    array = deviation * jax.random.normal(key, dims, jnp.float32)
    if shards:
        array = array * block_scale(key, dims, shards, -0.22, 0.18)
    return jnp.clip(raised(array, jax.random.fold_in(key, 3), *heavy), -most, most).astype(kind)


def setup_inputs(seed: int = 0, part: int = 0) -> dict:
    splits = jax.random.split(jax.random.key(seed), 6)
    part_splits = jax.random.split(jax.random.fold_in(splits[5], part), 6)
    return {
        "chol_full": bell_draw(splits[0], (NCH, N, N), (N * NCH) ** -0.5, 0.015625, ((1, 16),)),
        "chol_half": bell_draw(splits[1], (NCH, N, NOCC), (N * NOCC // 16) ** -0.5, 0.046875, ((1, 16),)),
        "green": noise_with(part_splits[2], (WALKERS, N, NOCC), 1.0, 6.0, ((1, 16),), (1, 0, 16, 2.0)),
        "gauss": bell_draw(part_splits[3], (WALKERS, NCH), 1.0, 5.0, (), jnp.float32),
        "orbitals": bell_draw(part_splits[4], (WALKERS, N, NOCC), 1.0, 6.0, ((0, 16),)),
    }


def reference(chol_full, chol_half, green, gauss, orbitals):
    walkers = green.shape[0]
    vbias = jnp.dot(green.reshape(walkers, -1), chol_half.reshape(NCH, -1).T, preferred_element_type=jnp.float32)
    xbar = jnp.clip(-0.3 * vbias, -1.0, 1.0)
    log_factor = jnp.sum(gauss * xbar - 0.5 * xbar * xbar, axis=1)
    fields = (gauss - xbar).astype(jnp.bfloat16)
    flat_chol = chol_full.reshape(NCH, N * N)

    def advance(item):
        field_row, orbit = item
        potential = (jnp.dot(field_row[None, :], flat_chol, preferred_element_type=jnp.float32) * 0.3).astype(jnp.bfloat16)
        potential = potential.reshape(N, N)
        moved = jnp.dot(potential, orbit, preferred_element_type=jnp.float32)
        return (orbit.astype(jnp.float32) + moved).astype(jnp.bfloat16)

    new_orbitals = lax.map(advance, (fields, orbitals))
    return new_orbitals, log_factor
```

```python
import functools

import jax
import jax.numpy as jnp
from jax import lax
from jax.experimental import pallas as pl
from jax.experimental.pallas import tpu as pltpu
from jax.sharding import PartitionSpec as P

TILE = 16
LANES = 128


def remote(src, dst, send, recv, peer):
    return pltpu.make_async_remote_copy(
        src_ref=src,
        dst_ref=dst,
        send_sem=send,
        recv_sem=recv,
        device_id={"chol": peer},
        device_id_type=pl.DeviceIdType.MESH,
    )


def kernel(
    n, chol_hbm, half_hbm, green_hbm, gauss_ref, orb_ref,
    out_ref, log_ref,
    chol, half, green, part, part_in, fields_own, fields_in, send, recv,
    load_sem, aux_sem, part_send, part_recv, field_send, field_recv, pot_send, pot_recv,
):
    me = lax.axis_index("chol")
    owned = part.shape[1]
    tiles = chol.shape[0]
    width = chol.shape[3]

    half_copy = pltpu.make_async_copy(half_hbm, half, aux_sem.at[0])
    green_copy = pltpu.make_async_copy(green_hbm, green, aux_sem.at[1])
    half_copy.start()
    green_copy.start()
    loads = [
        pltpu.make_async_copy(chol_hbm.at[:, pl.ds(t * TILE, TILE), :], chol.at[t], load_sem.at[t])
        for t in range(tiles)
    ]
    for load in loads:
        load.start()

    barrier = pltpu.get_barrier_semaphore()

    def greet(k, _):
        pl.semaphore_signal(
            barrier, inc=1, device_id={"chol": lax.rem(me + k, n)}, device_id_type=pl.DeviceIdType.MESH
        )
        return 0

    lax.fori_loop(1, n, greet, 0)

    half_copy.wait()
    green_copy.wait()

    def bias(t, acc):
        rows = pl.ds(pl.multiple_of(t * TILE, TILE), TILE)
        left = jnp.swapaxes(green[:, rows, :], 0, 1)
        right = jnp.swapaxes(half[:, rows, :], 0, 1)
        for r in range(TILE):
            acc += lax.dot_general(
                left[r], right[r], (((1,), (1,)), ((), ())), preferred_element_type=jnp.float32
            )
        return acc

    total = lax.fori_loop(0, tiles, bias, jnp.zeros((n * owned, half.shape[0]), jnp.float32))
    for d in range(n):
        part[d] = total[d * owned:(d + 1) * owned]
    pl.semaphore_wait(barrier, n - 1)

    def peer_of(k):
        return lax.rem(me + k, n)

    def push_part(k, _):
        to = peer_of(k)
        remote(part.at[to], part_in.at[me], part_send.at[to], part_recv.at[me], to).start()
        return 0

    lax.fori_loop(1, n, push_part, 0)
    part_in[me] = part[me]

    def wait_part(k, _):
        peer = peer_of(k)
        copy = remote(part.at[peer], part_in.at[peer], part_send.at[peer], part_recv.at[peer], peer)
        copy.wait_recv()
        return 0

    lax.fori_loop(1, n, wait_part, 0)
    vbias = jnp.sum(part_in[...], axis=0)
    gauss = gauss_ref[me]
    xbar = jnp.clip(-0.3 * vbias, -1.0, 1.0)
    log_ref[...] = jnp.broadcast_to(
        jnp.sum(gauss * xbar - 0.5 * xbar * xbar, axis=1, keepdims=True), log_ref.shape
    )
    mine = gauss - xbar
    fields_own[...] = mine
    fields_in[me] = mine

    def push_field(k, _):
        to = peer_of(k)
        remote(fields_own, fields_in.at[me], field_send.at[to], field_recv.at[me], to).start()
        return 0

    lax.fori_loop(1, n, push_field, 0)

    def wait_field(k, _):
        peer = peer_of(k)
        remote(fields_own, fields_in.at[peer], field_send.at[peer], field_recv.at[peer], peer).wait_recv()
        return 0

    lax.fori_loop(1, n, wait_field, 0)
    fields = jnp.concatenate([fields_in[d] for d in range(n)], axis=0).astype(jnp.bfloat16)

    def walkers_of(d):
        return pl.ds(d * owned, owned)

    def rows_of(d):
        return pl.ds(pl.multiple_of(d * TILE, TILE), TILE)

    for t in range(tiles):
        loads[t].wait()

        def strip(c, _):
            cols = pl.ds(pl.multiple_of(c * LANES, LANES), LANES)
            block = jnp.swapaxes(chol[t, :, :, cols], 0, 1)
            pots = [
                (jnp.dot(fields, block[r], preferred_element_type=jnp.float32) * 0.3).astype(jnp.bfloat16)
                for r in range(TILE)
            ]
            send[t, :, :, cols] = jnp.swapaxes(jnp.stack(pots, axis=0), 0, 1)
            return 0

        lax.fori_loop(0, width // LANES, strip, 0)

        def push_pot(k, _):
            to = peer_of(k)
            remote(
                send.at[t, walkers_of(to)], recv.at[t, :, rows_of(me), :],
                pot_send.at[t, to], pot_recv.at[t, me], to,
            ).start()
            return 0

        lax.fori_loop(1, n, push_pot, 0)
        recv[t, :, rows_of(me), :] = send[t, walkers_of(me)]

    for t in range(tiles):

        def wait_pot(k, _):
            peer = peer_of(k)
            remote(
                send.at[t, walkers_of(peer)], recv.at[t, :, rows_of(peer), :],
                pot_send.at[t, peer], pot_recv.at[t, peer], peer,
            ).wait_recv()
            return 0

        lax.fori_loop(1, n, wait_pot, 0)

        def advance(w, _):
            orbit = orb_ref[w].reshape(width, orb_ref.shape[-1])
            for first in range(0, n, 16):
                span = min(16, n - first)
                moved = jnp.dot(
                    recv[t, w, first * TILE:(first + span) * TILE, :], orbit,
                    preferred_element_type=jnp.float32,
                ).reshape(span, TILE, orbit.shape[-1])
                old = orb_ref[w, first:first + span, t].astype(jnp.float32)
                out_ref[w, first:first + span, t] = (old + moved).astype(jnp.bfloat16)
            return 0

        lax.fori_loop(0, owned, advance, 0)

    def drain(k, _):
        peer = peer_of(k)
        remote(part.at[peer], part_in.at[peer], part_send.at[peer], part_recv.at[peer], peer).wait_send()
        remote(fields_own, fields_in.at[peer], field_send.at[peer], field_recv.at[peer], peer).wait_send()
        for t in range(tiles):
            remote(
                send.at[t, walkers_of(peer)], recv.at[t, :, rows_of(peer), :],
                pot_send.at[t, peer], pot_recv.at[t, peer], peer,
            ).wait_send()
        return 0

    lax.fori_loop(1, n, drain, 0)


def on_device(n, chol_full, chol_half, green, gauss, orbitals):
    walkers, local_rows, nocc = green.shape
    owned, width, _ = orbitals.shape
    vectors = chol_half.shape[0]
    tiles = local_rows // TILE
    vmem = pl.BlockSpec(memory_space=pltpu.VMEM)
    hbm = pl.BlockSpec(memory_space=pl.ANY)
    dma = pltpu.SemaphoreType.DMA
    split = (owned, n, tiles, TILE, nocc)
    moved, logs = pl.pallas_call(
        functools.partial(kernel, n),
        out_shape=(
            jax.ShapeDtypeStruct(split, jnp.bfloat16),
            jax.ShapeDtypeStruct((owned, LANES), jnp.float32),
        ),
        in_specs=[hbm, hbm, hbm, vmem, vmem],
        out_specs=(vmem, vmem),
        scratch_shapes=[
            pltpu.VMEM((tiles, vectors, TILE, width), jnp.bfloat16),
            pltpu.VMEM((vectors, local_rows, nocc), jnp.bfloat16),
            pltpu.VMEM((walkers, local_rows, nocc), jnp.bfloat16),
            pltpu.VMEM((n, owned, vectors), jnp.float32),
            pltpu.VMEM((n, owned, vectors), jnp.float32),
            pltpu.VMEM((owned, vectors), jnp.float32),
            pltpu.VMEM((n, owned, vectors), jnp.float32),
            pltpu.VMEM((tiles, walkers, TILE, width), jnp.bfloat16),
            pltpu.VMEM((tiles, owned, n * TILE, width), jnp.bfloat16),
            dma((tiles,)), dma((2,)), dma((n,)), dma((n,)), dma((n,)), dma((n,)),
            dma((tiles, n)), dma((tiles, n)),
        ],
        compiler_params=pltpu.CompilerParams(
            collective_id=0, has_side_effects=True, vmem_limit_bytes=60 << 20
        ),
    )(chol_full, chol_half, green, gauss.reshape(n, owned, vectors), orbitals.reshape(split))
    return moved.reshape(orbitals.shape), logs[:, 0]


def solution(mesh):
    placed = (
        P(None, "chol", None),
        P(None, "chol", None),
        P("grp", "chol", None),
        P("grp", None),
        P(("grp", "chol"), None, None),
    )
    return jax.shard_map(
        functools.partial(on_device, mesh.shape["chol"]),
        mesh=mesh,
        in_specs=placed,
        out_specs=(P(("grp", "chol"), None, None), P(("grp", "chol"))),
        check_vma=False,
    )
```

```python
import functools

import jax
import jax.numpy as jnp
from jax import lax
from jax.experimental import pallas as pl
from jax.experimental.pallas import tpu as pltpu
from jax.sharding import PartitionSpec as P

TILE = 16
LANES = 128
PLANE = 4
GUEST_LIMIT = 16 << 20


def remote(src, dst, send, recv, peer):
    return pltpu.make_async_remote_copy(
        src_ref=src,
        dst_ref=dst,
        send_sem=send,
        recv_sem=recv,
        device_id={"chol": peer},
        device_id_type=pl.DeviceIdType.MESH,
    )


def direct_kernel(
    n, chol_hbm, half_hbm, green_hbm, gauss_ref, orb_ref,
    out_ref, log_ref,
    chol, half, green, part, part_in, fields_own, fields_in, send, recv,
    load_sem, aux_sem, part_send, part_recv, field_send, field_recv, pot_send, pot_recv,
):
    me = lax.axis_index("chol")
    owned = part.shape[1]
    tiles = chol.shape[0]
    width = chol.shape[3]

    half_copy = pltpu.make_async_copy(half_hbm, half, aux_sem.at[0])
    green_copy = pltpu.make_async_copy(green_hbm, green, aux_sem.at[1])
    half_copy.start()
    green_copy.start()
    loads = [
        pltpu.make_async_copy(chol_hbm.at[:, pl.ds(t * TILE, TILE), :], chol.at[t], load_sem.at[t])
        for t in range(tiles)
    ]
    for load in loads:
        load.start()

    barrier = pltpu.get_barrier_semaphore()

    def greet(k, _):
        pl.semaphore_signal(
            barrier, inc=1, device_id={"chol": lax.rem(me + k, n)}, device_id_type=pl.DeviceIdType.MESH
        )
        return 0

    lax.fori_loop(1, n, greet, 0)

    half_copy.wait()
    green_copy.wait()

    def bias(t, acc):
        rows = pl.ds(pl.multiple_of(t * TILE, TILE), TILE)
        left = jnp.swapaxes(green[:, rows, :], 0, 1)
        right = jnp.swapaxes(half[:, rows, :], 0, 1)
        for r in range(TILE):
            acc += lax.dot_general(
                left[r], right[r], (((1,), (1,)), ((), ())), preferred_element_type=jnp.float32
            )
        return acc

    total = lax.fori_loop(0, tiles, bias, jnp.zeros((n * owned, half.shape[0]), jnp.float32))
    for d in range(n):
        part[d] = total[d * owned:(d + 1) * owned]
    pl.semaphore_wait(barrier, n - 1)

    def peer_of(k):
        return lax.rem(me + k, n)

    def push_part(k, _):
        to = peer_of(k)
        remote(part.at[to], part_in.at[me], part_send.at[to], part_recv.at[me], to).start()
        return 0

    lax.fori_loop(1, n, push_part, 0)
    part_in[me] = part[me]

    def wait_part(k, _):
        peer = peer_of(k)
        copy = remote(part.at[peer], part_in.at[peer], part_send.at[peer], part_recv.at[peer], peer)
        copy.wait_recv()
        return 0

    lax.fori_loop(1, n, wait_part, 0)
    vbias = jnp.sum(part_in[...], axis=0)
    gauss = gauss_ref[me]
    xbar = jnp.clip(-0.3 * vbias, -1.0, 1.0)
    log_ref[...] = jnp.broadcast_to(
        jnp.sum(gauss * xbar - 0.5 * xbar * xbar, axis=1, keepdims=True), log_ref.shape
    )
    mine = gauss - xbar
    fields_own[...] = mine
    fields_in[me] = mine

    def push_field(k, _):
        to = peer_of(k)
        remote(fields_own, fields_in.at[me], field_send.at[to], field_recv.at[me], to).start()
        return 0

    lax.fori_loop(1, n, push_field, 0)

    def wait_field(k, _):
        peer = peer_of(k)
        remote(fields_own, fields_in.at[peer], field_send.at[peer], field_recv.at[peer], peer).wait_recv()
        return 0

    lax.fori_loop(1, n, wait_field, 0)
    fields = jnp.concatenate([fields_in[d] for d in range(n)], axis=0).astype(jnp.bfloat16)

    def walkers_of(d):
        return pl.ds(d * owned, owned)

    def rows_of(d):
        return pl.ds(pl.multiple_of(d * TILE, TILE), TILE)

    for t in range(tiles):
        loads[t].wait()

        def strip(c, _):
            cols = pl.ds(pl.multiple_of(c * LANES, LANES), LANES)
            block = jnp.swapaxes(chol[t, :, :, cols], 0, 1)
            pots = [
                (jnp.dot(fields, block[r], preferred_element_type=jnp.float32) * 0.3).astype(jnp.bfloat16)
                for r in range(TILE)
            ]
            send[t, :, :, cols] = jnp.swapaxes(jnp.stack(pots, axis=0), 0, 1)
            return 0

        lax.fori_loop(0, width // LANES, strip, 0)

        def push_pot(k, _):
            to = peer_of(k)
            remote(
                send.at[t, walkers_of(to)], recv.at[t, :, rows_of(me), :],
                pot_send.at[t, to], pot_recv.at[t, me], to,
            ).start()
            return 0

        lax.fori_loop(1, n, push_pot, 0)
        recv[t, :, rows_of(me), :] = send[t, walkers_of(me)]

    for t in range(tiles):

        def wait_pot(k, _):
            peer = peer_of(k)
            remote(
                send.at[t, walkers_of(peer)], recv.at[t, :, rows_of(peer), :],
                pot_send.at[t, peer], pot_recv.at[t, peer], peer,
            ).wait_recv()
            return 0

        lax.fori_loop(1, n, wait_pot, 0)

        def advance(w, _):
            orbit = orb_ref[w].reshape(width, orb_ref.shape[-1])
            for first in range(0, n, 16):
                span = min(16, n - first)
                moved = jnp.dot(
                    recv[t, w, first * TILE:(first + span) * TILE, :], orbit,
                    preferred_element_type=jnp.float32,
                ).reshape(span, TILE, orbit.shape[-1])
                old = orb_ref[w, first:first + span, t].astype(jnp.float32)
                out_ref[w, first:first + span, t] = (old + moved).astype(jnp.bfloat16)
            return 0

        lax.fori_loop(0, owned, advance, 0)

    def drain(k, _):
        peer = peer_of(k)
        remote(part.at[peer], part_in.at[peer], part_send.at[peer], part_recv.at[peer], peer).wait_send()
        remote(fields_own, fields_in.at[peer], field_send.at[peer], field_recv.at[peer], peer).wait_send()
        for t in range(tiles):
            remote(
                send.at[t, walkers_of(peer)], recv.at[t, :, rows_of(peer), :],
                pot_send.at[t, peer], pot_recv.at[t, peer], peer,
            ).wait_send()
        return 0

    lax.fori_loop(1, n, drain, 0)


def relay_kernel(
    n, chol_hbm, half_hbm, green_hbm, gauss_ref, orb_ref,
    out_ref, log_ref,
    chol, half, green, part, part_in, fields_own, fields_in, send, recv, guest, done,
    load_sem, aux_sem, part_send, part_recv, field_send, field_recv, pot_send, pot_recv,
    own_send, guest_recv, relay_send, pass_send, done_send, done_recv,
):
    me = lax.axis_index("chol")
    owned = part.shape[1]
    tiles = chol.shape[0]
    width = chol.shape[3]

    half_copy = pltpu.make_async_copy(half_hbm, half, aux_sem.at[0])
    green_copy = pltpu.make_async_copy(green_hbm, green, aux_sem.at[1])
    half_copy.start()
    green_copy.start()
    loads = [
        pltpu.make_async_copy(chol_hbm.at[:, pl.ds(t * TILE, TILE), :], chol.at[t], load_sem.at[t])
        for t in range(tiles)
    ]
    for load in loads:
        load.start()

    barrier = pltpu.get_barrier_semaphore()

    def greet(k, _):
        pl.semaphore_signal(
            barrier, inc=1, device_id={"chol": lax.rem(me + k, n)}, device_id_type=pl.DeviceIdType.MESH
        )
        return 0

    lax.fori_loop(1, n, greet, 0)

    half_copy.wait()
    green_copy.wait()

    def bias(t, acc):
        rows = pl.ds(pl.multiple_of(t * TILE, TILE), TILE)
        left = jnp.swapaxes(green[:, rows, :], 0, 1)
        right = jnp.swapaxes(half[:, rows, :], 0, 1)
        for r in range(TILE):
            acc += lax.dot_general(
                left[r], right[r], (((1,), (1,)), ((), ())), preferred_element_type=jnp.float32
            )
        return acc

    total = lax.fori_loop(0, tiles, bias, jnp.zeros((n * owned, half.shape[0]), jnp.float32))
    for d in range(n):
        part[d] = total[d * owned:(d + 1) * owned]
    pl.semaphore_wait(barrier, n - 1)

    def peer_of(k):
        return lax.rem(me + k, n)

    def push_part(k, _):
        to = peer_of(k)
        remote(part.at[to], part_in.at[me], part_send.at[to], part_recv.at[me], to).start()
        return 0

    lax.fori_loop(1, n, push_part, 0)
    part_in[me] = part[me]

    def wait_part(k, _):
        peer = peer_of(k)
        copy = remote(part.at[peer], part_in.at[peer], part_send.at[peer], part_recv.at[peer], peer)
        copy.wait_recv()
        return 0

    lax.fori_loop(1, n, wait_part, 0)
    vbias = jnp.sum(part_in[...], axis=0)
    gauss = gauss_ref[me]
    xbar = jnp.clip(-0.3 * vbias, -1.0, 1.0)
    log_ref[...] = jnp.broadcast_to(
        jnp.sum(gauss * xbar - 0.5 * xbar * xbar, axis=1, keepdims=True), log_ref.shape
    )
    mine = gauss - xbar
    fields_own[...] = mine
    fields_in[me] = mine

    def push_field(k, _):
        to = peer_of(k)
        remote(fields_own, fields_in.at[me], field_send.at[to], field_recv.at[me], to).start()
        return 0

    lax.fori_loop(1, n, push_field, 0)

    def wait_field(k, _):
        peer = peer_of(k)
        remote(fields_own, fields_in.at[peer], field_send.at[peer], field_recv.at[peer], peer).wait_recv()
        return 0

    lax.fori_loop(1, n, wait_field, 0)
    fields = jnp.concatenate([fields_in[d] for d in range(n)], axis=0).astype(jnp.bfloat16)

    def walkers_of(d):
        return pl.ds(d * owned, owned)

    def rows_of(d):
        return pl.ds(pl.multiple_of(d * TILE, TILE), TILE)

    near = n // 2
    planes = near // PLANE
    mine_at = lax.rem(me, near)
    home = me - mine_at
    away = near - home
    seat = lax.rem(me, PLANE)
    across = lax.rem(seat + 2, PLANE)
    upper = me // near
    entry = away + (1 - upper) * 0 + upper * (near - PLANE) + seat
    depth = upper * (mine_at // PLANE) + (1 - upper) * (planes - 1 - mine_at // PLANE)
    outward = lax.rem(me + n + (2 * upper - 1) * PLANE, n)
    partner = me + 1 - 2 * lax.rem(me, 2)
    beside = me - seat + across

    def swap(j):
        return j + 1 - 2 * lax.rem(j, 2)

    def guest_copy(slot, w, sem, to):
        return remote(guest.at[slot, w], guest.at[slot, w], sem, guest_recv.at[slot, w], to)

    def host(w):
        return remote(orb_ref.at[w], guest.at[mine_at, w], own_send.at[w], guest_recv.at[mine_at, w], entry)

    for w in range(owned):
        host(w).start()

    def fill(t):
        loads[t].wait()

        def strip(c, _):
            cols = pl.ds(pl.multiple_of(c * LANES, LANES), LANES)
            block = jnp.swapaxes(chol[t, :, :, cols], 0, 1)
            pots = [
                (jnp.dot(fields, block[r], preferred_element_type=jnp.float32) * 0.3).astype(jnp.bfloat16)
                for r in range(TILE)
            ]
            send[t, :, :, cols] = jnp.swapaxes(jnp.stack(pots, axis=0), 0, 1)
            return 0

        lax.fori_loop(0, width // LANES, strip, 0)
        recv[t, :, rows_of(mine_at), :] = send[t, walkers_of(me)]

    def fellow(k):
        return lax.rem(mine_at + k, near)

    def pot_copy(t, there, source):
        return remote(
            send.at[t, walkers_of(home + there)], recv.at[t, :, rows_of(source), :],
            pot_send.at[t, there], pot_recv.at[t, source], home + there,
        )

    def push(t):
        def step(k, _):
            pot_copy(t, fellow(k), mine_at).start()
            return 0

        lax.fori_loop(1, near, step, 0)

    def column(oz):
        return oz * PLANE + seat

    def relay(w):
        for oz in range(planes):
            slot = column(oz)
            guest_copy(slot, w, own_send.at[w], partner).wait_recv()

            @pl.when(depth < planes - 1)
            def _():
                guest_copy(slot, w, relay_send.at[0, oz, w], outward).start()

            guest_copy(slot, w, relay_send.at[1, oz, w], beside).start()
            guest_copy(slot, w, relay_send.at[2, oz, w], partner).start()

    def hand_over(w):
        for oz in range(planes):
            slot = oz * PLANE + across
            guest_copy(slot, w, own_send.at[w], partner).wait_recv()
            guest_copy(slot, w, pass_send.at[oz, w], partner).start()

    def done_copy(slot, w):
        return remote(
            done.at[slot, w], out_ref.at[w, me], done_send.at[slot, w], done_recv.at[mine_at, w], away + slot
        )

    def serve(slot, w):
        left = send[:, (away + slot) * owned + w].reshape(tiles * TILE, width)
        orbit = guest[slot, w].reshape(width, guest.shape[-1])
        moved = jnp.dot(left, orbit, preferred_element_type=jnp.float32)
        old = guest[slot, w, me].astype(jnp.float32)
        done[slot, w] = (old + moved.reshape(old.shape)).astype(jnp.bfloat16)
        done_copy(slot, w).start()

    def serve_column(w, j, wait):
        for oz in range(planes):
            slot = oz * PLANE + j
            if wait:
                guest_copy(slot, w, own_send.at[w], partner).wait_recv()
            serve(slot, w)

    for t in range(tiles):
        fill(t)
        if t == 0:
            push(0)
    for w in range(owned + 1):
        if w < owned:
            relay(w)
        if w == owned - 1 or (w < owned and w + 1 >= tiles):
            for t in range(w + 1, tiles):
                push(t)
        elif w < owned:
            push(w + 1)
        if w > 0:
            hand_over(w - 1)
        if w < owned:
            serve_column(w, seat, False)
            serve_column(w, swap(seat), True)
        if w > 0:
            serve_column(w - 1, across, False)
            serve_column(w - 1, swap(across), True)

    for t in range(tiles):

        def wait_pot(k, _):
            source = fellow(k)
            pot_copy(t, source, source).wait_recv()
            return 0

        lax.fori_loop(1, near, wait_pot, 0)

        def advance(w, _):
            orbit = orb_ref[w].reshape(width, orb_ref.shape[-1])
            moved = jnp.dot(recv[t, w], orbit, preferred_element_type=jnp.float32)
            rows = pl.ds(home, near)
            old = orb_ref[w, rows, t].astype(jnp.float32)
            out_ref[w, rows, t] = (old + moved.reshape(old.shape)).astype(jnp.bfloat16)
            return 0

        lax.fori_loop(0, owned, advance, 0)

    def drain(k, _):
        peer = peer_of(k)
        remote(part.at[peer], part_in.at[peer], part_send.at[peer], part_recv.at[peer], peer).wait_send()
        remote(fields_own, fields_in.at[peer], field_send.at[peer], field_recv.at[peer], peer).wait_send()
        return 0

    lax.fori_loop(1, n, drain, 0)

    def drain_pot(k, _):
        for t in range(tiles):
            pot_copy(t, fellow(k), mine_at).wait_send()
        return 0

    lax.fori_loop(1, near, drain_pot, 0)
    for w in range(owned):
        host(w).wait_send()
        for oz in range(planes):
            slot = column(oz)

            @pl.when(depth < planes - 1)
            def _():
                guest_copy(slot, w, relay_send.at[0, oz, w], outward).wait_send()

            guest_copy(slot, w, relay_send.at[1, oz, w], beside).wait_send()
            guest_copy(slot, w, relay_send.at[2, oz, w], partner).wait_send()
            guest_copy(oz * PLANE + across, w, pass_send.at[oz, w], partner).wait_send()

    def collect(slot, _):
        for w in range(owned):
            done_copy(slot, w).wait_send()
            remote(
                done.at[slot, w], out_ref.at[w, away + slot], done_send.at[slot, w], done_recv.at[slot, w], away + slot
            ).wait_recv()
        return 0

    lax.fori_loop(0, near, collect, 0)


def on_device(n, chol_full, chol_half, green, gauss, orbitals):
    walkers, local_rows, nocc = green.shape
    owned, width, _ = orbitals.shape
    vectors = chol_half.shape[0]
    tiles = local_rows // TILE
    vmem = pl.BlockSpec(memory_space=pltpu.VMEM)
    hbm = pl.BlockSpec(memory_space=pl.ANY)
    dma = pltpu.SemaphoreType.DMA
    split = (owned, n, tiles, TILE, nocc)
    near = n // 2
    guests = near * orbitals.size * orbitals.dtype.itemsize
    relayed = n % (2 * PLANE) == 0 and guests <= GUEST_LIMIT
    peers = near if relayed else n
    extra, extra_sems = [], []
    if relayed:
        planes = near // PLANE
        extra = [
            pltpu.VMEM((near,) + split, jnp.bfloat16),
            pltpu.VMEM((near, owned, tiles, TILE, nocc), jnp.bfloat16),
        ]
        extra_sems = [
            dma((owned,)), dma((near, owned)), dma((3, planes, owned)), dma((planes, owned)),
            dma((near, owned)), dma((near, owned)),
        ]
    moved, logs = pl.pallas_call(
        functools.partial(relay_kernel if relayed else direct_kernel, n),
        out_shape=(
            jax.ShapeDtypeStruct(split, jnp.bfloat16),
            jax.ShapeDtypeStruct((owned, LANES), jnp.float32),
        ),
        in_specs=[hbm, hbm, hbm, vmem, vmem],
        out_specs=(vmem, vmem),
        scratch_shapes=[
            pltpu.VMEM((tiles, vectors, TILE, width), jnp.bfloat16),
            pltpu.VMEM((vectors, local_rows, nocc), jnp.bfloat16),
            pltpu.VMEM((walkers, local_rows, nocc), jnp.bfloat16),
            pltpu.VMEM((n, owned, vectors), jnp.float32),
            pltpu.VMEM((n, owned, vectors), jnp.float32),
            pltpu.VMEM((owned, vectors), jnp.float32),
            pltpu.VMEM((n, owned, vectors), jnp.float32),
            pltpu.VMEM((tiles, walkers, TILE, width), jnp.bfloat16),
            pltpu.VMEM((tiles, owned, peers * TILE, width), jnp.bfloat16),
            *extra,
            dma((tiles,)), dma((2,)), dma((n,)), dma((n,)), dma((n,)), dma((n,)),
            dma((tiles, peers)), dma((tiles, peers)), *extra_sems,
        ],
        compiler_params=pltpu.CompilerParams(
            collective_id=0, has_side_effects=True, vmem_limit_bytes=60 << 20
        ),
    )(chol_full, chol_half, green, gauss.reshape(n, owned, vectors), orbitals.reshape(split))
    return moved.reshape(orbitals.shape), logs[:, 0]


def solution(mesh):
    placed = (
        P(None, "chol", None),
        P(None, "chol", None),
        P("grp", "chol", None),
        P("grp", None),
        P(("grp", "chol"), None, None),
    )
    return jax.shard_map(
        functools.partial(on_device, mesh.shape["chol"]),
        mesh=mesh,
        in_specs=placed,
        out_specs=(P(("grp", "chol"), None, None), P(("grp", "chol"))),
        check_vma=False,
    )
```

```python
import functools

import jax
import jax.numpy as jnp
from jax import lax
from jax.experimental import pallas as pl
from jax.experimental.pallas import tpu as pltpu
from jax.sharding import PartitionSpec as P

TILE = 16
LANES = 128
PLANE = 4
GUEST_LIMIT = 16 << 20


def remote(src, dst, send, recv, peer):
    return pltpu.make_async_remote_copy(
        src_ref=src,
        dst_ref=dst,
        send_sem=send,
        recv_sem=recv,
        device_id={"chol": peer},
        device_id_type=pl.DeviceIdType.MESH,
    )


def direct_kernel(
    n, chol_hbm, half_hbm, green_hbm, gauss_ref, orb_ref,
    out_ref, log_ref,
    chol, half, green, part, part_in, fields_own, fields_in, send, recv,
    load_sem, aux_sem, part_send, part_recv, field_send, field_recv, pot_send, pot_recv,
):
    me = lax.axis_index("chol")
    owned = part.shape[1]
    tiles = chol.shape[0]
    width = chol.shape[3]

    half_copy = pltpu.make_async_copy(half_hbm, half, aux_sem.at[0])
    green_copy = pltpu.make_async_copy(green_hbm, green, aux_sem.at[1])
    half_copy.start()
    green_copy.start()
    loads = [
        pltpu.make_async_copy(chol_hbm.at[:, pl.ds(t * TILE, TILE), :], chol.at[t], load_sem.at[t])
        for t in range(tiles)
    ]
    for load in loads:
        load.start()

    barrier = pltpu.get_barrier_semaphore()

    def greet(k, _):
        pl.semaphore_signal(
            barrier, inc=1, device_id={"chol": lax.rem(me + k, n)}, device_id_type=pl.DeviceIdType.MESH
        )
        return 0

    lax.fori_loop(1, n, greet, 0)

    half_copy.wait()
    green_copy.wait()

    def bias(t, acc):
        rows = pl.ds(pl.multiple_of(t * TILE, TILE), TILE)
        left = jnp.swapaxes(green[:, rows, :], 0, 1)
        right = jnp.swapaxes(half[:, rows, :], 0, 1)
        for r in range(TILE):
            acc += lax.dot_general(
                left[r], right[r], (((1,), (1,)), ((), ())), preferred_element_type=jnp.float32
            )
        return acc

    total = lax.fori_loop(0, tiles, bias, jnp.zeros((n * owned, half.shape[0]), jnp.float32))
    for d in range(n):
        part[d] = total[d * owned:(d + 1) * owned]
    pl.semaphore_wait(barrier, n - 1)

    def peer_of(k):
        return lax.rem(me + k, n)

    def push_part(k, _):
        to = peer_of(k)
        remote(part.at[to], part_in.at[me], part_send.at[to], part_recv.at[me], to).start()
        return 0

    lax.fori_loop(1, n, push_part, 0)
    part_in[me] = part[me]

    def wait_part(k, _):
        peer = peer_of(k)
        copy = remote(part.at[peer], part_in.at[peer], part_send.at[peer], part_recv.at[peer], peer)
        copy.wait_recv()
        return 0

    lax.fori_loop(1, n, wait_part, 0)
    vbias = jnp.sum(part_in[...], axis=0)
    gauss = gauss_ref[me]
    xbar = jnp.clip(-0.3 * vbias, -1.0, 1.0)
    log_ref[...] = jnp.broadcast_to(
        jnp.sum(gauss * xbar - 0.5 * xbar * xbar, axis=1, keepdims=True), log_ref.shape
    )
    mine = gauss - xbar
    fields_own[...] = mine
    fields_in[me] = mine

    def push_field(k, _):
        to = peer_of(k)
        remote(fields_own, fields_in.at[me], field_send.at[to], field_recv.at[me], to).start()
        return 0

    lax.fori_loop(1, n, push_field, 0)

    def wait_field(k, _):
        peer = peer_of(k)
        remote(fields_own, fields_in.at[peer], field_send.at[peer], field_recv.at[peer], peer).wait_recv()
        return 0

    lax.fori_loop(1, n, wait_field, 0)
    fields = jnp.concatenate([fields_in[d] for d in range(n)], axis=0).astype(jnp.bfloat16)

    def walkers_of(d):
        return pl.ds(d * owned, owned)

    def rows_of(d):
        return pl.ds(pl.multiple_of(d * TILE, TILE), TILE)

    for t in range(tiles):
        loads[t].wait()

        def strip(c, _):
            cols = pl.ds(pl.multiple_of(c * LANES, LANES), LANES)
            block = jnp.swapaxes(chol[t, :, :, cols], 0, 1)
            pots = [
                (jnp.dot(fields, block[r], preferred_element_type=jnp.float32) * 0.3).astype(jnp.bfloat16)
                for r in range(TILE)
            ]
            send[t, :, :, cols] = jnp.swapaxes(jnp.stack(pots, axis=0), 0, 1)
            return 0

        lax.fori_loop(0, width // LANES, strip, 0)

        def push_pot(k, _):
            to = peer_of(k)
            remote(
                send.at[t, walkers_of(to)], recv.at[t, :, rows_of(me), :],
                pot_send.at[t, to], pot_recv.at[t, me], to,
            ).start()
            return 0

        lax.fori_loop(1, n, push_pot, 0)
        recv[t, :, rows_of(me), :] = send[t, walkers_of(me)]

    for t in range(tiles):

        def wait_pot(k, _):
            peer = peer_of(k)
            remote(
                send.at[t, walkers_of(peer)], recv.at[t, :, rows_of(peer), :],
                pot_send.at[t, peer], pot_recv.at[t, peer], peer,
            ).wait_recv()
            return 0

        lax.fori_loop(1, n, wait_pot, 0)

        def advance(w, _):
            orbit = orb_ref[w].reshape(width, orb_ref.shape[-1])
            for first in range(0, n, 16):
                span = min(16, n - first)
                moved = jnp.dot(
                    recv[t, w, first * TILE:(first + span) * TILE, :], orbit,
                    preferred_element_type=jnp.float32,
                ).reshape(span, TILE, orbit.shape[-1])
                old = orb_ref[w, first:first + span, t].astype(jnp.float32)
                out_ref[w, first:first + span, t] = (old + moved).astype(jnp.bfloat16)
            return 0

        lax.fori_loop(0, owned, advance, 0)

    def drain(k, _):
        peer = peer_of(k)
        remote(part.at[peer], part_in.at[peer], part_send.at[peer], part_recv.at[peer], peer).wait_send()
        remote(fields_own, fields_in.at[peer], field_send.at[peer], field_recv.at[peer], peer).wait_send()
        for t in range(tiles):
            remote(
                send.at[t, walkers_of(peer)], recv.at[t, :, rows_of(peer), :],
                pot_send.at[t, peer], pot_recv.at[t, peer], peer,
            ).wait_send()
        return 0

    lax.fori_loop(1, n, drain, 0)


def relay_kernel(
    n, chol_hbm, half_hbm, green_hbm, gauss_ref, orb_ref,
    out_ref, log_ref,
    chol, half, green, part, part_in, fields_own, fields_in, send, recv, guest, done, hop,
    load_sem, aux_sem, part_send, part_recv, field_send, field_recv, pot_send, pot_recv,
    own_send, guest_recv, relay_send, pass_send, done_send, done_recv, hop_send, hop_recv,
):
    me = lax.axis_index("chol")
    owned = part.shape[1]
    tiles = chol.shape[0]
    width = chol.shape[3]

    half_copy = pltpu.make_async_copy(half_hbm, half, aux_sem.at[0])
    green_copy = pltpu.make_async_copy(green_hbm, green, aux_sem.at[1])
    half_copy.start()
    green_copy.start()
    loads = [
        pltpu.make_async_copy(chol_hbm.at[:, pl.ds(t * TILE, TILE), :], chol.at[t], load_sem.at[t])
        for t in range(tiles)
    ]
    for load in loads:
        load.start()

    barrier = pltpu.get_barrier_semaphore()

    def greet(k, _):
        pl.semaphore_signal(
            barrier, inc=1, device_id={"chol": lax.rem(me + k, n)}, device_id_type=pl.DeviceIdType.MESH
        )
        return 0

    lax.fori_loop(1, n, greet, 0)

    half_copy.wait()
    green_copy.wait()

    def bias(t, acc):
        rows = pl.ds(pl.multiple_of(t * TILE, TILE), TILE)
        left = jnp.swapaxes(green[:, rows, :], 0, 1)
        right = jnp.swapaxes(half[:, rows, :], 0, 1)
        for r in range(TILE):
            acc += lax.dot_general(
                left[r], right[r], (((1,), (1,)), ((), ())), preferred_element_type=jnp.float32
            )
        return acc

    total = lax.fori_loop(0, tiles, bias, jnp.zeros((n * owned, half.shape[0]), jnp.float32))
    for d in range(n):
        part[d] = total[d * owned:(d + 1) * owned]
    pl.semaphore_wait(barrier, n - 1)

    def peer_of(k):
        return lax.rem(me + k, n)

    def push_part(k, _):
        to = peer_of(k)
        remote(part.at[to], part_in.at[me], part_send.at[to], part_recv.at[me], to).start()
        return 0

    lax.fori_loop(1, n, push_part, 0)
    part_in[me] = part[me]

    def wait_part(k, _):
        peer = peer_of(k)
        copy = remote(part.at[peer], part_in.at[peer], part_send.at[peer], part_recv.at[peer], peer)
        copy.wait_recv()
        return 0

    lax.fori_loop(1, n, wait_part, 0)
    vbias = jnp.sum(part_in[...], axis=0)
    gauss = gauss_ref[me]
    xbar = jnp.clip(-0.3 * vbias, -1.0, 1.0)
    log_ref[...] = jnp.broadcast_to(
        jnp.sum(gauss * xbar - 0.5 * xbar * xbar, axis=1, keepdims=True), log_ref.shape
    )
    mine = gauss - xbar
    fields_own[...] = mine
    fields_in[me] = mine

    def push_field(k, _):
        to = peer_of(k)
        remote(fields_own, fields_in.at[me], field_send.at[to], field_recv.at[me], to).start()
        return 0

    lax.fori_loop(1, n, push_field, 0)

    def wait_field(k, _):
        peer = peer_of(k)
        remote(fields_own, fields_in.at[peer], field_send.at[peer], field_recv.at[peer], peer).wait_recv()
        return 0

    lax.fori_loop(1, n, wait_field, 0)
    fields = jnp.concatenate([fields_in[d] for d in range(n)], axis=0).astype(jnp.bfloat16)

    def walkers_of(d):
        return pl.ds(d * owned, owned)

    def rows_of(d):
        return pl.ds(pl.multiple_of(d * TILE, TILE), TILE)

    near = n // 2
    planes = near // PLANE
    mine_at = lax.rem(me, near)
    home = me - mine_at
    away = near - home
    seat = lax.rem(me, PLANE)
    across = lax.rem(seat + 2, PLANE)
    upper = me // near
    entry = away + (1 - upper) * 0 + upper * (near - PLANE) + seat
    depth = upper * (mine_at // PLANE) + (1 - upper) * (planes - 1 - mine_at // PLANE)
    outward = lax.rem(me + n + (2 * upper - 1) * PLANE, n)
    inward = lax.rem(me + n - (2 * upper - 1) * PLANE, n)
    partner = me + 1 - 2 * lax.rem(me, 2)
    beside = me - seat + across

    def swap(j):
        return j + 1 - 2 * lax.rem(j, 2)

    def guest_copy(slot, w, sem, to):
        return remote(guest.at[slot, w], guest.at[slot, w], sem, guest_recv.at[slot, w], to)

    inner = depth == 0
    outer = depth > 0
    behind = lax.rem(outward, near)

    def host(w):
        return remote(orb_ref.at[w], guest.at[mine_at, w], own_send.at[w], guest_recv.at[mine_at, w], entry)

    def lift(w):
        return remote(orb_ref.at[w], hop.at[w], own_send.at[w], hop_recv.at[w], inward)

    def onward(w):
        return remote(hop.at[w], guest.at[behind, w], hop_send.at[w], guest_recv.at[behind, w], entry)

    @pl.when(inner)
    def _():
        for w in range(owned):
            host(w).start()

    @pl.when(outer)
    def _():
        for w in range(owned):
            lift(w).start()

    def forward(w):
        @pl.when(inner)
        def _():
            lift(w).wait_recv()
            onward(w).start()

    def fill(t):
        loads[t].wait()

        def strip(c, _):
            cols = pl.ds(pl.multiple_of(c * LANES, LANES), LANES)
            block = jnp.swapaxes(chol[t, :, :, cols], 0, 1)
            pots = [
                (jnp.dot(fields, block[r], preferred_element_type=jnp.float32) * 0.3).astype(jnp.bfloat16)
                for r in range(TILE)
            ]
            send[t, :, :, cols] = jnp.swapaxes(jnp.stack(pots, axis=0), 0, 1)
            return 0

        lax.fori_loop(0, width // LANES, strip, 0)
        recv[t, :, rows_of(mine_at), :] = send[t, walkers_of(me)]

    def fellow(k):
        return lax.rem(mine_at + k, near)

    def pot_copy(t, there, source):
        return remote(
            send.at[t, walkers_of(home + there)], recv.at[t, :, rows_of(source), :],
            pot_send.at[t, there], pot_recv.at[t, source], home + there,
        )

    def push(t):
        def step(k, _):
            pot_copy(t, fellow(k), mine_at).start()
            return 0

        lax.fori_loop(1, near, step, 0)

    first = away // near

    def block(s):
        oz = s // owned
        return (oz + (1 - 2 * oz) * (1 - first), s % owned)

    def relay(s):
        oz, w = block(s)
        slot = oz * PLANE + seat
        guest_copy(slot, w, own_send.at[w], partner).wait_recv()

        @pl.when(inner)
        def _():
            guest_copy(slot, w, relay_send.at[0, s], outward).start()

        guest_copy(slot, w, relay_send.at[1, s], beside).start()
        guest_copy(slot, w, relay_send.at[2, s], partner).start()

    def hand_over(s):
        oz, w = block(s)
        slot = oz * PLANE + across
        guest_copy(slot, w, own_send.at[w], partner).wait_recv()
        guest_copy(slot, w, pass_send.at[s], partner).start()

    def done_copy(slot, w):
        return remote(
            done.at[slot, w], out_ref.at[w, me], done_send.at[slot, w], done_recv.at[mine_at, w], away + slot
        )

    def serve(slot, w):
        left = send[:, (away + slot) * owned + w].reshape(tiles * TILE, width)
        orbit = guest[slot, w].reshape(width, guest.shape[-1])
        moved = jnp.dot(left, orbit, preferred_element_type=jnp.float32)
        old = guest[slot, w, me].astype(jnp.float32)
        done[slot, w] = (old + moved.reshape(old.shape)).astype(jnp.bfloat16)
        done_copy(slot, w).start()

    def serve_block(s, j, wait):
        oz, w = block(s)
        slot = oz * PLANE + j
        if wait:
            guest_copy(slot, w, own_send.at[w], partner).wait_recv()
        serve(slot, w)

    steps = planes * owned
    early = tiles // 2
    for t in range(tiles):
        fill(t)
        if t < early:
            push(t)
    for s in range(steps + 2):
        if s < owned:
            forward(s)
        if s < steps:
            relay(s)
        if s == steps - 1:
            for t in range(early, tiles):
                push(t)
        if 0 < s <= steps:
            hand_over(s - 1)
        if s < steps:
            serve_block(s, seat, False)
            serve_block(s, swap(seat), True)
        if s > 1:
            serve_block(s - 2, across, False)
            serve_block(s - 2, swap(across), True)

    for t in range(tiles):

        def wait_pot(k, _):
            source = fellow(k)
            pot_copy(t, source, source).wait_recv()
            return 0

        lax.fori_loop(1, near, wait_pot, 0)

        def advance(w, _):
            orbit = orb_ref[w].reshape(width, orb_ref.shape[-1])
            moved = jnp.dot(recv[t, w], orbit, preferred_element_type=jnp.float32)
            rows = pl.ds(home, near)
            old = orb_ref[w, rows, t].astype(jnp.float32)
            out_ref[w, rows, t] = (old + moved.reshape(old.shape)).astype(jnp.bfloat16)
            return 0

        lax.fori_loop(0, owned, advance, 0)

    def drain(k, _):
        peer = peer_of(k)
        remote(part.at[peer], part_in.at[peer], part_send.at[peer], part_recv.at[peer], peer).wait_send()
        remote(fields_own, fields_in.at[peer], field_send.at[peer], field_recv.at[peer], peer).wait_send()
        return 0

    lax.fori_loop(1, n, drain, 0)

    def drain_pot(k, _):
        for t in range(tiles):
            pot_copy(t, fellow(k), mine_at).wait_send()
        return 0

    lax.fori_loop(1, near, drain_pot, 0)
    for w in range(owned):
        host(w).wait_send()

        @pl.when(inner)
        def _():
            onward(w).wait_send()

    for s in range(steps):
        oz, w = block(s)
        slot = oz * PLANE + seat

        @pl.when(inner)
        def _():
            guest_copy(slot, w, relay_send.at[0, s], outward).wait_send()

        guest_copy(slot, w, relay_send.at[1, s], beside).wait_send()
        guest_copy(slot, w, relay_send.at[2, s], partner).wait_send()
        guest_copy(slot, w, pass_send.at[s], partner).wait_send()

    def collect(slot, _):
        for w in range(owned):
            done_copy(slot, w).wait_send()
            remote(
                done.at[slot, w], out_ref.at[w, away + slot], done_send.at[slot, w], done_recv.at[slot, w], away + slot
            ).wait_recv()
        return 0

    lax.fori_loop(0, near, collect, 0)


def on_device(n, chol_full, chol_half, green, gauss, orbitals):
    walkers, local_rows, nocc = green.shape
    owned, width, _ = orbitals.shape
    vectors = chol_half.shape[0]
    tiles = local_rows // TILE
    vmem = pl.BlockSpec(memory_space=pltpu.VMEM)
    hbm = pl.BlockSpec(memory_space=pl.ANY)
    dma = pltpu.SemaphoreType.DMA
    split = (owned, n, tiles, TILE, nocc)
    near = n // 2
    guests = near * orbitals.size * orbitals.dtype.itemsize
    relayed = n == 4 * PLANE and guests <= GUEST_LIMIT
    peers = near if relayed else n
    extra, extra_sems = [], []
    if relayed:
        planes = near // PLANE
        extra = [
            pltpu.VMEM((near,) + split, jnp.bfloat16),
            pltpu.VMEM((near, owned, tiles, TILE, nocc), jnp.bfloat16),
            pltpu.VMEM(split, jnp.bfloat16),
        ]
        extra_sems = [
            dma((owned,)), dma((near, owned)), dma((3, planes * owned)), dma((planes * owned,)),
            dma((near, owned)), dma((near, owned)), dma((owned,)), dma((owned,)),
        ]
    moved, logs = pl.pallas_call(
        functools.partial(relay_kernel if relayed else direct_kernel, n),
        out_shape=(
            jax.ShapeDtypeStruct(split, jnp.bfloat16),
            jax.ShapeDtypeStruct((owned, LANES), jnp.float32),
        ),
        in_specs=[hbm, hbm, hbm, vmem, vmem],
        out_specs=(vmem, vmem),
        scratch_shapes=[
            pltpu.VMEM((tiles, vectors, TILE, width), jnp.bfloat16),
            pltpu.VMEM((vectors, local_rows, nocc), jnp.bfloat16),
            pltpu.VMEM((walkers, local_rows, nocc), jnp.bfloat16),
            pltpu.VMEM((n, owned, vectors), jnp.float32),
            pltpu.VMEM((n, owned, vectors), jnp.float32),
            pltpu.VMEM((owned, vectors), jnp.float32),
            pltpu.VMEM((n, owned, vectors), jnp.float32),
            pltpu.VMEM((tiles, walkers, TILE, width), jnp.bfloat16),
            pltpu.VMEM((tiles, owned, peers * TILE, width), jnp.bfloat16),
            *extra,
            dma((tiles,)), dma((2,)), dma((n,)), dma((n,)), dma((n,)), dma((n,)),
            dma((tiles, peers)), dma((tiles, peers)), *extra_sems,
        ],
        compiler_params=pltpu.CompilerParams(
            collective_id=0, has_side_effects=True, vmem_limit_bytes=60 << 20
        ),
    )(chol_full, chol_half, green, gauss.reshape(n, owned, vectors), orbitals.reshape(split))
    return moved.reshape(orbitals.shape), logs[:, 0]


def solution(mesh):
    placed = (
        P(None, "chol", None),
        P(None, "chol", None),
        P("grp", "chol", None),
        P("grp", None),
        P(("grp", "chol"), None, None),
    )
    return jax.shard_map(
        functools.partial(on_device, mesh.shape["chol"]),
        mesh=mesh,
        in_specs=placed,
        out_specs=(P(("grp", "chol"), None, None), P(("grp", "chol"))),
        check_vma=False,
    )
```

```python
import functools

import jax
import jax.numpy as jnp
from jax import lax
from jax.experimental import pallas as pl
from jax.experimental.pallas import tpu as pltpu
from jax.sharding import PartitionSpec as P

TILE = 16
LANES = 128
PLANE = 4
GUEST_LIMIT = 16 << 20


def remote(src, dst, send, recv, peer):
    return pltpu.make_async_remote_copy(
        src_ref=src,
        dst_ref=dst,
        send_sem=send,
        recv_sem=recv,
        device_id={"chol": peer},
        device_id_type=pl.DeviceIdType.MESH,
    )


def direct_kernel(
    n, chol_hbm, half_hbm, green_hbm, gauss_ref, orb_ref,
    out_ref, log_ref,
    chol, half, green, part, part_in, fields_own, fields_in, send, recv,
    load_sem, aux_sem, part_send, part_recv, field_send, field_recv, pot_send, pot_recv,
):
    me = lax.axis_index("chol")
    owned = part.shape[1]
    tiles = chol.shape[0]
    width = chol.shape[3]

    half_copy = pltpu.make_async_copy(half_hbm, half, aux_sem.at[0])
    green_copy = pltpu.make_async_copy(green_hbm, green, aux_sem.at[1])
    half_copy.start()
    green_copy.start()
    loads = [
        pltpu.make_async_copy(chol_hbm.at[:, pl.ds(t * TILE, TILE), :], chol.at[t], load_sem.at[t])
        for t in range(tiles)
    ]
    for load in loads:
        load.start()

    barrier = pltpu.get_barrier_semaphore()

    def greet(k, _):
        pl.semaphore_signal(
            barrier, inc=1, device_id={"chol": lax.rem(me + k, n)}, device_id_type=pl.DeviceIdType.MESH
        )
        return 0

    lax.fori_loop(1, n, greet, 0)

    half_copy.wait()
    green_copy.wait()

    def bias(t, acc):
        rows = pl.ds(pl.multiple_of(t * TILE, TILE), TILE)
        left = jnp.swapaxes(green[:, rows, :], 0, 1)
        right = jnp.swapaxes(half[:, rows, :], 0, 1)
        for r in range(TILE):
            acc += lax.dot_general(
                left[r], right[r], (((1,), (1,)), ((), ())), preferred_element_type=jnp.float32
            )
        return acc

    total = lax.fori_loop(0, tiles, bias, jnp.zeros((n * owned, half.shape[0]), jnp.float32))
    for d in range(n):
        part[d] = total[d * owned:(d + 1) * owned]
    pl.semaphore_wait(barrier, n - 1)

    def peer_of(k):
        return lax.rem(me + k, n)

    def push_part(k, _):
        to = peer_of(k)
        remote(part.at[to], part_in.at[me], part_send.at[to], part_recv.at[me], to).start()
        return 0

    lax.fori_loop(1, n, push_part, 0)
    part_in[me] = part[me]

    def wait_part(k, _):
        peer = peer_of(k)
        copy = remote(part.at[peer], part_in.at[peer], part_send.at[peer], part_recv.at[peer], peer)
        copy.wait_recv()
        return 0

    lax.fori_loop(1, n, wait_part, 0)
    vbias = jnp.sum(part_in[...], axis=0)
    gauss = gauss_ref[me]
    xbar = jnp.clip(-0.3 * vbias, -1.0, 1.0)
    log_ref[...] = jnp.broadcast_to(
        jnp.sum(gauss * xbar - 0.5 * xbar * xbar, axis=1, keepdims=True), log_ref.shape
    )
    mine = gauss - xbar
    fields_own[...] = mine
    fields_in[me] = mine

    def push_field(k, _):
        to = peer_of(k)
        remote(fields_own, fields_in.at[me], field_send.at[to], field_recv.at[me], to).start()
        return 0

    lax.fori_loop(1, n, push_field, 0)

    def wait_field(k, _):
        peer = peer_of(k)
        remote(fields_own, fields_in.at[peer], field_send.at[peer], field_recv.at[peer], peer).wait_recv()
        return 0

    lax.fori_loop(1, n, wait_field, 0)
    fields = jnp.concatenate([fields_in[d] for d in range(n)], axis=0).astype(jnp.bfloat16)

    def walkers_of(d):
        return pl.ds(d * owned, owned)

    def rows_of(d):
        return pl.ds(pl.multiple_of(d * TILE, TILE), TILE)

    for t in range(tiles):
        loads[t].wait()

        def strip(c, _):
            cols = pl.ds(pl.multiple_of(c * LANES, LANES), LANES)
            block = jnp.swapaxes(chol[t, :, :, cols], 0, 1)
            pots = [
                (jnp.dot(fields, block[r], preferred_element_type=jnp.float32) * 0.3).astype(jnp.bfloat16)
                for r in range(TILE)
            ]
            send[t, :, :, cols] = jnp.swapaxes(jnp.stack(pots, axis=0), 0, 1)
            return 0

        lax.fori_loop(0, width // LANES, strip, 0)

        def push_pot(k, _):
            to = peer_of(k)
            remote(
                send.at[t, walkers_of(to)], recv.at[t, :, rows_of(me), :],
                pot_send.at[t, to], pot_recv.at[t, me], to,
            ).start()
            return 0

        lax.fori_loop(1, n, push_pot, 0)
        recv[t, :, rows_of(me), :] = send[t, walkers_of(me)]

    for t in range(tiles):

        def wait_pot(k, _):
            peer = peer_of(k)
            remote(
                send.at[t, walkers_of(peer)], recv.at[t, :, rows_of(peer), :],
                pot_send.at[t, peer], pot_recv.at[t, peer], peer,
            ).wait_recv()
            return 0

        lax.fori_loop(1, n, wait_pot, 0)

        def advance(w, _):
            orbit = orb_ref[w].reshape(width, orb_ref.shape[-1])
            for first in range(0, n, 16):
                span = min(16, n - first)
                moved = jnp.dot(
                    recv[t, w, first * TILE:(first + span) * TILE, :], orbit,
                    preferred_element_type=jnp.float32,
                ).reshape(span, TILE, orbit.shape[-1])
                old = orb_ref[w, first:first + span, t].astype(jnp.float32)
                out_ref[w, first:first + span, t] = (old + moved).astype(jnp.bfloat16)
            return 0

        lax.fori_loop(0, owned, advance, 0)

    def drain(k, _):
        peer = peer_of(k)
        remote(part.at[peer], part_in.at[peer], part_send.at[peer], part_recv.at[peer], peer).wait_send()
        remote(fields_own, fields_in.at[peer], field_send.at[peer], field_recv.at[peer], peer).wait_send()
        for t in range(tiles):
            remote(
                send.at[t, walkers_of(peer)], recv.at[t, :, rows_of(peer), :],
                pot_send.at[t, peer], pot_recv.at[t, peer], peer,
            ).wait_send()
        return 0

    lax.fori_loop(1, n, drain, 0)


def relay_kernel(
    n, chol_hbm, half_hbm, green_hbm, gauss_ref, orb_ref,
    out_ref, log_ref,
    chol, half, green, part, part_in, fields_own, fields_in, send, recv, guest, done, hop,
    load_sem, aux_sem, part_send, part_recv, field_send, field_recv, pot_send, pot_recv,
    own_send, guest_recv, relay_send, pass_send, done_send, done_recv, hop_send, hop_recv,
):
    me = lax.axis_index("chol")
    owned = part.shape[1]
    tiles = chol.shape[0]
    width = chol.shape[3]

    half_copy = pltpu.make_async_copy(half_hbm, half, aux_sem.at[0])
    green_copy = pltpu.make_async_copy(green_hbm, green, aux_sem.at[1])
    half_copy.start()
    green_copy.start()
    loads = [
        pltpu.make_async_copy(chol_hbm.at[:, pl.ds(t * TILE, TILE), :], chol.at[t], load_sem.at[t])
        for t in range(tiles)
    ]
    for load in loads:
        load.start()

    barrier = pltpu.get_barrier_semaphore()

    def greet(k, _):
        pl.semaphore_signal(
            barrier, inc=1, device_id={"chol": lax.rem(me + k, n)}, device_id_type=pl.DeviceIdType.MESH
        )
        return 0

    lax.fori_loop(1, n, greet, 0)

    half_copy.wait()
    green_copy.wait()

    def bias(t, acc):
        rows = pl.ds(pl.multiple_of(t * TILE, TILE), TILE)
        left = jnp.swapaxes(green[:, rows, :], 0, 1)
        right = jnp.swapaxes(half[:, rows, :], 0, 1)
        for r in range(TILE):
            acc += lax.dot_general(
                left[r], right[r], (((1,), (1,)), ((), ())), preferred_element_type=jnp.float32
            )
        return acc

    total = lax.fori_loop(0, tiles, bias, jnp.zeros((n * owned, half.shape[0]), jnp.float32))
    for d in range(n):
        part[d] = total[d * owned:(d + 1) * owned]
    pl.semaphore_wait(barrier, n - 1)

    def peer_of(k):
        return lax.rem(me + k, n)

    def push_part(k, _):
        to = peer_of(k)
        remote(part.at[to], part_in.at[me], part_send.at[to], part_recv.at[me], to).start()
        return 0

    lax.fori_loop(1, n, push_part, 0)
    part_in[me] = part[me]

    def wait_part(k, _):
        peer = peer_of(k)
        copy = remote(part.at[peer], part_in.at[peer], part_send.at[peer], part_recv.at[peer], peer)
        copy.wait_recv()
        return 0

    lax.fori_loop(1, n, wait_part, 0)
    vbias = jnp.sum(part_in[...], axis=0)
    gauss = gauss_ref[me]
    xbar = jnp.clip(-0.3 * vbias, -1.0, 1.0)
    log_ref[...] = jnp.broadcast_to(
        jnp.sum(gauss * xbar - 0.5 * xbar * xbar, axis=1, keepdims=True), log_ref.shape
    )
    mine = gauss - xbar
    fields_own[...] = mine
    fields_in[me] = mine

    def push_field(k, _):
        to = peer_of(k)
        remote(fields_own, fields_in.at[me], field_send.at[to], field_recv.at[me], to).start()
        return 0

    lax.fori_loop(1, n, push_field, 0)

    def wait_field(k, _):
        peer = peer_of(k)
        remote(fields_own, fields_in.at[peer], field_send.at[peer], field_recv.at[peer], peer).wait_recv()
        return 0

    lax.fori_loop(1, n, wait_field, 0)
    fields = jnp.concatenate([fields_in[d] for d in range(n)], axis=0).astype(jnp.bfloat16)

    def walkers_of(d):
        return pl.ds(d * owned, owned)

    def rows_of(d):
        return pl.ds(pl.multiple_of(d * TILE, TILE), TILE)

    near = n // 2
    planes = near // PLANE
    mine_at = lax.rem(me, near)
    home = me - mine_at
    away = near - home
    seat = lax.rem(me, PLANE)
    across = lax.rem(seat + 2, PLANE)
    upper = me // near
    entry = away + (1 - upper) * 0 + upper * (near - PLANE) + seat
    depth = upper * (mine_at // PLANE) + (1 - upper) * (planes - 1 - mine_at // PLANE)
    outward = lax.rem(me + n + (2 * upper - 1) * PLANE, n)
    inward = lax.rem(me + n - (2 * upper - 1) * PLANE, n)
    partner = me + 1 - 2 * lax.rem(me, 2)
    beside = me - seat + across

    def swap(j):
        return j + 1 - 2 * lax.rem(j, 2)

    def guest_copy(slot, w, sem, to):
        return remote(guest.at[slot, w], guest.at[slot, w], sem, guest_recv.at[slot, w], to)

    inner = depth == 0
    outer = depth > 0
    behind = lax.rem(outward, near)

    def host(w):
        return remote(orb_ref.at[w], guest.at[mine_at, w], own_send.at[w], guest_recv.at[mine_at, w], entry)

    def lift(w):
        return remote(orb_ref.at[w], hop.at[w], own_send.at[w], hop_recv.at[w], inward)

    def onward(w):
        return remote(hop.at[w], guest.at[behind, w], hop_send.at[w], guest_recv.at[behind, w], entry)

    @pl.when(inner)
    def _():
        for w in range(owned):
            host(w).start()

    @pl.when(outer)
    def _():
        for w in range(owned):
            lift(w).start()

    def forward(w):
        @pl.when(inner)
        def _():
            lift(w).wait_recv()
            onward(w).start()

    def fill(t):
        loads[t].wait()

        def strip(c, _):
            cols = pl.ds(pl.multiple_of(c * LANES, LANES), LANES)
            block = jnp.swapaxes(chol[t, :, :, cols], 0, 1)
            pots = [
                (jnp.dot(fields, block[r], preferred_element_type=jnp.float32) * 0.3).astype(jnp.bfloat16)
                for r in range(TILE)
            ]
            send[t, :, :, cols] = jnp.swapaxes(jnp.stack(pots, axis=0), 0, 1)
            return 0

        lax.fori_loop(0, width // LANES, strip, 0)
        recv[t, :, rows_of(mine_at), :] = send[t, walkers_of(me)]

    def fellow(k):
        return lax.rem(mine_at + k, near)

    def pot_copy(t, there, source):
        return remote(
            send.at[t, walkers_of(home + there)], recv.at[t, :, rows_of(source), :],
            pot_send.at[t, there], pot_recv.at[t, source], home + there,
        )

    def push(t):
        def step(k, _):
            pot_copy(t, fellow(k), mine_at).start()
            return 0

        lax.fori_loop(1, near, step, 0)

    first = away // near

    def block(s):
        oz = s // owned
        return (oz + (1 - 2 * oz) * (1 - first), s % owned)

    def relay(s):
        oz, w = block(s)
        slot = oz * PLANE + seat
        guest_copy(slot, w, own_send.at[w], partner).wait_recv()

        @pl.when(inner)
        def _():
            guest_copy(slot, w, relay_send.at[0, s], outward).start()

        guest_copy(slot, w, relay_send.at[1, s], beside).start()
        guest_copy(slot, w, relay_send.at[2, s], partner).start()

    def hand_over(s):
        oz, w = block(s)
        slot = oz * PLANE + across
        guest_copy(slot, w, own_send.at[w], partner).wait_recv()
        guest_copy(slot, w, pass_send.at[s], partner).start()

    def done_copy(slot, w):
        return remote(
            done.at[slot, w], out_ref.at[w, me], done_send.at[slot, w], done_recv.at[mine_at, w], away + slot
        )

    def serve(slot, w):
        left = send[:, (away + slot) * owned + w].reshape(tiles * TILE, width)
        orbit = guest[slot, w].reshape(width, guest.shape[-1])
        moved = jnp.dot(left, orbit, preferred_element_type=jnp.float32)
        old = guest[slot, w, me].astype(jnp.float32)
        done[slot, w] = (old + moved.reshape(old.shape)).astype(jnp.bfloat16)
        done_copy(slot, w).start()

    def serve_block(s, j, wait):
        oz, w = block(s)
        slot = oz * PLANE + j
        if wait:
            guest_copy(slot, w, own_send.at[w], partner).wait_recv()
        serve(slot, w)

    steps = planes * owned
    early = tiles - 1
    for t in range(tiles):
        fill(t)
        if t < early:
            push(t)
    for s in range(steps + 2):
        if s < owned:
            forward(s)
        if s < steps:
            relay(s)
        if s == steps - 1:
            for t in range(early, tiles):
                push(t)
        if 0 < s <= steps:
            hand_over(s - 1)
        if s < steps:
            serve_block(s, seat, False)
            serve_block(s, swap(seat), True)
        if s > 1:
            serve_block(s - 2, across, False)
            serve_block(s - 2, swap(across), True)

    for t in range(tiles):

        def wait_pot(k, _):
            source = fellow(k)
            pot_copy(t, source, source).wait_recv()
            return 0

        lax.fori_loop(1, near, wait_pot, 0)

        def advance(w, _):
            orbit = orb_ref[w].reshape(width, orb_ref.shape[-1])
            moved = jnp.dot(recv[t, w], orbit, preferred_element_type=jnp.float32)
            rows = pl.ds(home, near)
            old = orb_ref[w, rows, t].astype(jnp.float32)
            out_ref[w, rows, t] = (old + moved.reshape(old.shape)).astype(jnp.bfloat16)
            return 0

        lax.fori_loop(0, owned, advance, 0)

    def drain(k, _):
        peer = peer_of(k)
        remote(part.at[peer], part_in.at[peer], part_send.at[peer], part_recv.at[peer], peer).wait_send()
        remote(fields_own, fields_in.at[peer], field_send.at[peer], field_recv.at[peer], peer).wait_send()
        return 0

    lax.fori_loop(1, n, drain, 0)

    def drain_pot(k, _):
        for t in range(tiles):
            pot_copy(t, fellow(k), mine_at).wait_send()
        return 0

    lax.fori_loop(1, near, drain_pot, 0)
    for w in range(owned):
        host(w).wait_send()

        @pl.when(inner)
        def _():
            onward(w).wait_send()

    for s in range(steps):
        oz, w = block(s)
        slot = oz * PLANE + seat

        @pl.when(inner)
        def _():
            guest_copy(slot, w, relay_send.at[0, s], outward).wait_send()

        guest_copy(slot, w, relay_send.at[1, s], beside).wait_send()
        guest_copy(slot, w, relay_send.at[2, s], partner).wait_send()
        guest_copy(slot, w, pass_send.at[s], partner).wait_send()

    def collect(slot, _):
        for w in range(owned):
            done_copy(slot, w).wait_send()
            remote(
                done.at[slot, w], out_ref.at[w, away + slot], done_send.at[slot, w], done_recv.at[slot, w], away + slot
            ).wait_recv()
        return 0

    lax.fori_loop(0, near, collect, 0)


def on_device(n, chol_full, chol_half, green, gauss, orbitals):
    walkers, local_rows, nocc = green.shape
    owned, width, _ = orbitals.shape
    vectors = chol_half.shape[0]
    tiles = local_rows // TILE
    vmem = pl.BlockSpec(memory_space=pltpu.VMEM)
    hbm = pl.BlockSpec(memory_space=pl.ANY)
    dma = pltpu.SemaphoreType.DMA
    split = (owned, n, tiles, TILE, nocc)
    near = n // 2
    guests = near * orbitals.size * orbitals.dtype.itemsize
    relayed = n == 4 * PLANE and guests <= GUEST_LIMIT
    peers = near if relayed else n
    extra, extra_sems = [], []
    if relayed:
        planes = near // PLANE
        extra = [
            pltpu.VMEM((near,) + split, jnp.bfloat16),
            pltpu.VMEM((near, owned, tiles, TILE, nocc), jnp.bfloat16),
            pltpu.VMEM(split, jnp.bfloat16),
        ]
        extra_sems = [
            dma((owned,)), dma((near, owned)), dma((3, planes * owned)), dma((planes * owned,)),
            dma((near, owned)), dma((near, owned)), dma((owned,)), dma((owned,)),
        ]
    moved, logs = pl.pallas_call(
        functools.partial(relay_kernel if relayed else direct_kernel, n),
        out_shape=(
            jax.ShapeDtypeStruct(split, jnp.bfloat16),
            jax.ShapeDtypeStruct((owned, LANES), jnp.float32),
        ),
        in_specs=[hbm, hbm, hbm, vmem, vmem],
        out_specs=(vmem, vmem),
        scratch_shapes=[
            pltpu.VMEM((tiles, vectors, TILE, width), jnp.bfloat16),
            pltpu.VMEM((vectors, local_rows, nocc), jnp.bfloat16),
            pltpu.VMEM((walkers, local_rows, nocc), jnp.bfloat16),
            pltpu.VMEM((n, owned, vectors), jnp.float32),
            pltpu.VMEM((n, owned, vectors), jnp.float32),
            pltpu.VMEM((owned, vectors), jnp.float32),
            pltpu.VMEM((n, owned, vectors), jnp.float32),
            pltpu.VMEM((tiles, walkers, TILE, width), jnp.bfloat16),
            pltpu.VMEM((tiles, owned, peers * TILE, width), jnp.bfloat16),
            *extra,
            dma((tiles,)), dma((2,)), dma((n,)), dma((n,)), dma((n,)), dma((n,)),
            dma((tiles, peers)), dma((tiles, peers)), *extra_sems,
        ],
        compiler_params=pltpu.CompilerParams(
            collective_id=0, has_side_effects=True, vmem_limit_bytes=60 << 20
        ),
    )(chol_full, chol_half, green, gauss.reshape(n, owned, vectors), orbitals.reshape(split))
    return moved.reshape(orbitals.shape), logs[:, 0]


def solution(mesh):
    placed = (
        P(None, "chol", None),
        P(None, "chol", None),
        P("grp", "chol", None),
        P("grp", None),
        P(("grp", "chol"), None, None),
    )
    return jax.shard_map(
        functools.partial(on_device, mesh.shape["chol"]),
        mesh=mesh,
        in_specs=placed,
        out_specs=(P(("grp", "chol"), None, None), P(("grp", "chol"))),
        check_vma=False,
    )
```
